256 devices in a mesh: ta: 64 (over y, z, x_hi), gz: 4 (over x_lo, core).
Axes of the slice: x: 4 (x_hi: 2, x_lo: 2; x = x_hi * 2 + x_lo), y: 4, z: 8, core: 2. Of those that a mesh axis runs over, the one named last changes fastest.
Arguments:
- eigvecs: bfloat16 [64, 2, 3, 16, 256, 128], P('ta', None, None, 'gz'), may hold values from -6 to 6
- gauge_links: bfloat16 [64, 3, 3, 3, 2, 16, 256], P('ta', None, None, None, None, 'gz'), may hold values from -2.5 to 2.5
- peramb: bfloat16 [64, 4, 4, 4, 2, 128, 128], P('ta', None, 'gz'), may hold values from -0.3984375 to 0.3984375
- momenta: int32 [2, 3], replicated, may hold values from -2 to 2
- disp_paths: int32 [2, 2], replicated, may hold values from 1 to 3, as said below
- sources: int32 [4], replicated, may hold values from 0 to 63
Outputs:
- elementals: bfloat16 [64, 2, 2, 2, 128, 128], P('ta', None, None, None, 'gz')
- correlator: float32 [4, 64, 2, 2, 2], P(None, 'ta')
The draws below stay inside these ranges and needn't reach their ends.
Inputs may be any that keep to these rules, and one draw needn't show every extreme that they name: `disp_paths`: in each momentum's row exactly one path runs along the third dimension (value 3); every other path is 1 or 2.
All inputs are finite; a program needn't handle non-finite values.
Results may differ from the reference program's by a relative error of at most 0.0081.
Values may be sent and summed in bfloat16 or wider, within the bound.
No kernel may reach another device: no remote copies, remote signals or barrier semaphores. Data moves between devices by JAX's collectives and lax.ppermute only.
A program may use at most 128 MiB of HBM per device.

```python
import math
import jax
import jax.numpy as jnp
from jax import lax

NVEC = 128
LX = 16
LY = 16
NMOM = 2
NDISP = 2
NSRC = 4
NT = 64
LZ = 16
LXY = 256


def draw_disp_paths(key, part):
    chosen = jax.random.randint(jax.random.fold_in(key, 11), (NMOM, 1), 0, NDISP)
    others = jax.random.randint(jax.random.fold_in(key, 12), (NMOM, NDISP), 1, 3)
    slots = jnp.arange(NDISP, dtype=jnp.int32)[None, :]
    return jnp.where(slots == chosen, 3, others).astype(jnp.int32)


def plant(result, rng, low, top_value):
    longest = result.shape.index(max(result.shape))
    spots = []
    for shift in (0, 1):
        where = [jax.random.randint(jax.random.fold_in(rng, axis), (), 0, length) for axis, length in enumerate(result.shape)]
        where[longest] = (where[longest] + shift) % result.shape[longest]
        spots.append(tuple(where))
    return result.at[spots[0]].set(low).at[spots[1]].set(top_value)


def levels(key, shape, split, low, top_value):
    level = 1.0
    for dim, parts in split:
        steps = jax.random.uniform(jax.random.fold_in(jax.random.fold_in(key, 6), dim), (parts,), jnp.float32, low / len(split), top_value / len(split))
        level = level * jnp.repeat(jnp.exp(steps), shape[dim] // parts).reshape((-1,) + (1,) * (len(shape) - 1 - dim))
    return level


def noise(rng, dims, scale, reach, split=(), held_as=jnp.bfloat16):
    loudness = levels(rng, dims, split, -0.22, 0.18) if split else 1.0
    array = jax.random.normal(rng, dims, jnp.float32) * scale * loudness
    return jnp.minimum(jnp.maximum(array, -reach), reach).astype(held_as)


def setup_inputs(seed: int = 0) -> dict:
    streams_of = jax.random.split(jax.random.key(seed), 7)
    return {
        "eigvecs": noise(streams_of[0], (NT, 2, 3, LZ, LXY, NVEC), 1.0, 6.0, ((0, 64), (3, 4))),
        "gauge_links": noise(streams_of[1], (NT, 3, 3, 3, 2, LZ, LXY), 0.408, 2.5, ((0, 64), (5, 4))),
        "peramb": noise(streams_of[2], (NT, NSRC, 4, 4, 2, NVEC, NVEC), 0.0625, 0.3984375, ((0, 64), (2, 4))),
        "momenta": plant(jax.random.randint(streams_of[3], (NMOM, 3), -2, 3), jax.random.fold_in(streams_of[3], 1), -2, 2).astype(jnp.int32),
        "disp_paths": draw_disp_paths(jax.random.fold_in(streams_of[6], 71), 0),
        "sources": plant(jax.random.randint(streams_of[5], (NSRC,), 0, NT), jax.random.fold_in(streams_of[5], 1), 0, NT - 1).astype(jnp.int32),
    }


HIGHEST = lax.Precision.HIGHEST

def transport(link_dir, source):
    link_re = link_dir[:, :, 0].astype(jnp.float32)
    link_im = link_dir[:, :, 1].astype(jnp.float32)
    source_re = source[0].astype(jnp.float32)
    source_im = source[1].astype(jnp.float32)
    total_re = jnp.zeros(source_re.shape, jnp.float32)
    total_im = jnp.zeros(source_re.shape, jnp.float32)
    for colour in range(3):
        coef_re = link_re[:, colour][..., None]
        coef_im = link_im[:, colour][..., None]
        total_re = total_re + coef_re * source_re[colour][None] - coef_im * source_im[colour][None]
        total_im = total_im + coef_re * source_im[colour][None] + coef_im * source_re[colour][None]
    return jnp.stack([total_re, total_im])

def back_transport(link_dir, source):
    link_re = link_dir[:, :, 0].astype(jnp.float32)
    link_im = link_dir[:, :, 1].astype(jnp.float32)
    source_re = source[0].astype(jnp.float32)
    source_im = source[1].astype(jnp.float32)
    total_re = jnp.zeros(source_re.shape, jnp.float32)
    total_im = jnp.zeros(source_re.shape, jnp.float32)
    for colour in range(3):
        coef_re = link_re[colour][..., None]
        coef_im = link_im[colour][..., None]
        total_re = total_re + coef_re * source_re[colour][None] + coef_im * source_im[colour][None]
        total_im = total_im + coef_re * source_im[colour][None] - coef_im * source_re[colour][None]
    return jnp.stack([total_re, total_im])

def displaced_fields(vectors, links_slice):
    results = []
    for direction in range(3):
        axis_id = (3, 4, 2)[direction]
        link_dir = links_slice[direction]
        shifted_up = jnp.roll(vectors, -1, axis=axis_id)
        forward = transport(link_dir, shifted_up)
        backward = back_transport(link_dir, vectors).astype(jnp.bfloat16)
        behind = jnp.roll(backward, 1, axis=axis_id).astype(jnp.float32)
        results.append((forward - behind).astype(jnp.bfloat16))
    return jnp.stack(results)

def phase_table(momentum, zcoord, lz_total):
    xcoord = jnp.arange(LX, dtype=jnp.int32)
    ycoord = jnp.arange(LY, dtype=jnp.int32)
    volume = LX * LY * lz_total
    phase_int = momentum[0] * xcoord[None, :, None] * (LY * lz_total) + momentum[1] * ycoord[None, None, :] * (LX * lz_total) + momentum[2] * zcoord[:, None, None] * (LX * LY)
    phase_int = jnp.mod(phase_int, volume)
    angles = phase_int.astype(jnp.float32) * (2.0 * math.pi / volume)
    return (jnp.cos(angles), jnp.sin(angles))

def elementals_one(vectors, selected, momentum, zcoord, lz_total):
    cosine, sine_table = phase_table(momentum, zcoord, lz_total)
    cosine = cosine[None, :, :, :, None]
    sine_table = sine_table[None, :, :, :, None]
    vec_re = vectors[0].astype(jnp.float32)
    vec_im = vectors[1].astype(jnp.float32)
    phased = jnp.stack([vec_re * cosine - vec_im * sine_table, -(vec_re * sine_table + vec_im * cosine)]).astype(jnp.bfloat16)
    num_vec = vectors.shape[-1]
    phased_rows = phased.reshape(2, -1, num_vec)
    displaced_cols = selected.reshape(selected.shape[0], 2, -1, num_vec)
    products = jnp.einsum('asi,dbsj->aidbj', phased_rows.astype(jnp.float32), displaced_cols.astype(jnp.float32), precision=HIGHEST)
    real_part = products[0, :, :, 0] - products[1, :, :, 1]
    imag_part = products[0, :, :, 1] + products[1, :, :, 0]
    return jnp.transpose(jnp.stack([real_part, imag_part]), (2, 0, 1, 3))

def slice_elementals(vectors_flat, links_flat, momenta, disp_paths):
    vectors = vectors_flat.reshape(2, 3, LZ, LX, LY, NVEC)
    links_slice = links_flat.reshape(3, 3, 3, 2, LZ, LX, LY)
    displaced = displaced_fields(vectors, links_slice)
    zcoord = jnp.arange(LZ, dtype=jnp.int32)

    def one_momentum(pair):
        selected = jnp.take(displaced, pair[1] - 1, axis=0)
        return elementals_one(vectors, selected, pair[0], zcoord, LZ)
    partial_value = lax.map(one_momentum, (momenta, disp_paths))
    norm_scale = 1.0 / math.sqrt(12.0 * LX * LY * LZ)
    return (partial_value * norm_scale).astype(jnp.bfloat16)

def contraction(sink_phi, source_phi, peramb_slice):
    sink_side = jnp.einsum('mdail,kpqblj->mdaikpqbj', sink_phi.astype(jnp.float32), peramb_slice.astype(jnp.float32), precision=HIGHEST)
    sink_re = sink_side[:, :, 0, :, :, :, :, 0] - sink_side[:, :, 1, :, :, :, :, 1]
    sink_im = sink_side[:, :, 0, :, :, :, :, 1] + sink_side[:, :, 1, :, :, :, :, 0]
    source_side = jnp.einsum('kpqail,kmdblj->kpqaimdbj', peramb_slice.astype(jnp.float32), source_phi.astype(jnp.float32), precision=HIGHEST)
    image_re = source_side[:, :, :, 0, :, :, :, 0] - source_side[:, :, :, 1, :, :, :, 1]
    image_im = source_side[:, :, :, 0, :, :, :, 1] + source_side[:, :, :, 1, :, :, :, 0]
    real_sum = jnp.einsum('mdikabj,kabimdj->kmd', sink_re, image_re, precision=HIGHEST) + jnp.einsum('mdikabj,kabimdj->kmd', sink_im, image_im, precision=HIGHEST)
    imag_sum = jnp.einsum('mdikabj,kabimdj->kmd', sink_im, image_re, precision=HIGHEST) - jnp.einsum('mdikabj,kabimdj->kmd', sink_re, image_im, precision=HIGHEST)
    return jnp.stack([real_sum, imag_sum], axis=-1)

def reference(eigvecs, gauge_links, peramb, momenta, disp_paths, sources):
    elementals = lax.map(lambda slice_pair: slice_elementals(slice_pair[0], slice_pair[1], momenta, disp_paths), (eigvecs, gauge_links))
    source_phi = jnp.take(elementals, sources, axis=0)

    def one_sink(slice_pair):
        return contraction(slice_pair[0], source_phi, slice_pair[1])
    corr_terms = lax.map(one_sink, (elementals, peramb))
    correlator = jnp.transpose(corr_terms, (1, 0, 2, 3, 4)) / (8.0 * NVEC)
    return (elementals, correlator)
```

```python
import functools
import math

import jax
import jax.numpy as jnp
import numpy as np
from jax import lax
from jax.experimental import pallas as pl
from jax.experimental.pallas import tpu as pltpu
from jax.sharding import Mesh
from jax.sharding import PartitionSpec as P

LX = 16
LY = 16
NSRC = 4
BF = jnp.bfloat16
F32 = jnp.float32
NT_DIMS = (((1,), (1,)), ((), ()))
TA = ("y", "z", "xh")
YZ = ("y", "z")
GZ = ("xl", "c")


def dot_nt(a, b):
    return lax.dot_general(a, b, NT_DIMS, preferred_element_type=F32)


def dot_nn(a, b):
    return jnp.dot(a, b, preferred_element_type=F32)


def shift_matrix(direction):
    row = lax.broadcasted_iota(jnp.int32, (256, 256), 0)
    col = lax.broadcasted_iota(jnp.int32, (256, 256), 1)
    if direction == 0:
        target = (col + LY) & 255
    else:
        target = (col & ~(LY - 1)) | ((col + 1) & (LY - 1))
    return jnp.where(row == target, 1.0, 0.0).astype(F32).astype(BF)


def unit_matrix(n):
    row = lax.broadcasted_iota(jnp.int32, (n, n), 0)
    col = lax.broadcasted_iota(jnp.int32, (n, n), 1)
    return jnp.where(row == col, 1.0, 0.0).astype(F32).astype(BF)


def transport(links, z, direction, source, target):
    for half in range(2):
        lanes = pl.ds(half * 128, 128)
        coef = [
            [
                [
                    jnp.broadcast_to(
                        links[z, pl.ds(direction * 18 + a * 6 + b * 2 + part, 1), lanes], (8, 128)
                    )
                    for part in range(2)
                ]
                for b in range(3)
            ]
            for a in range(3)
        ]

        def rows(step, _):
            parts = []
            for sub in range(2):
                at = pl.ds(pl.multiple_of(step * 16 + sub * 8, 8), 8)
                vec = [[source(part * 3 + b, at, lanes) for b in range(3)] for part in range(2)]
                out = []
                for a in range(3):
                    re = im = None
                    for b in range(3):
                        ur, ui = coef[a][b]
                        tr = ur * vec[0][b] - ui * vec[1][b]
                        ti = ur * vec[1][b] + ui * vec[0][b]
                        re = tr if re is None else re + tr
                        im = ti if im is None else im + ti
                    out.append((re, im))
                parts.append(out)
            for a in range(3):
                for part in range(2):
                    block = jnp.concatenate([parts[0][a][part], parts[1][a][part]], axis=0)
                    target[
                        pl.ds(pl.multiple_of(part * 128 + step * 16, 16), 16),
                        pl.ds(a * 256 + half * 128, 128),
                    ] = block.astype(BF)
            return 0

        lax.fori_loop(0, 8, rows, 0, unroll=2)


def phase_rows(ints, row, plane):
    site = lax.broadcasted_iota(jnp.int32, (8, 256), 1)
    x1 = site >> 4
    x2 = site & (LY - 1)
    steps = ints[row * 3] * x1 + ints[row * 3 + 1] * x2 + ints[row * 3 + 2] * plane
    angle = (steps & 15).astype(F32) * (2.0 * math.pi / 16.0)
    return jnp.cos(angle), jnp.sin(angle)


def local_kernel(ints, eig, links, acc, phased, vt, vs, field, perm):
    unit = unit_matrix(128)
    perm[0] = shift_matrix(0)
    perm[1] = shift_matrix(1)

    def load(z, _):
        for comp in range(6):
            vt[z, comp] = dot_nt(unit, eig[comp // 3, comp % 3, z])
        return 0

    lax.fori_loop(0, 4, load, 0)
    acc[...] = jnp.zeros_like(acc)

    def plane(z, _):
        for m in range(2):
            cosine, sine = phase_rows(ints, m, ints[10] + z)

            def rows(step, _):
                at = pl.ds(pl.multiple_of(step * 16, 16), 16)
                for half in range(2):
                    lanes = pl.ds(half * 128, 128)
                    cs = jnp.concatenate([cosine[:, half * 128 : half * 128 + 128]] * 2, axis=0)
                    sn = jnp.concatenate([sine[:, half * 128 : half * 128 + 128]] * 2, axis=0)
                    for a in range(3):
                        re = vt[z, a, at, lanes]
                        im = vt[z, 3 + a, at, lanes]
                        rc, rs, ic, js = re * cs, re * sn, im * cs, im * sn
                        to = pl.ds(a * 256 + half * 128, 128)
                        for block, value in enumerate((rc - js, -(rs + ic), rc + js, rs - ic)):
                            phased[
                                m, pl.ds(pl.multiple_of(block * 128 + step * 16, 16), 16), to
                            ] = value.astype(BF)
                return 0

            lax.fori_loop(0, 8, rows, 0)
        for direction in range(2):
            vs[...] = dot_nn(vt[z].reshape(768, 256).astype(BF), perm[direction]).reshape(
                6, 128, 256
            )
            transport(
                links, z, direction, lambda comp, at, lanes: vs[comp, at, lanes], field.at[direction]
            )
        for m in range(2):
            which = jnp.where(ints[6 + 2 * m] == 3, ints[7 + 2 * m], ints[6 + 2 * m]) - 1
            acc[2 * m + 1] += dot_nt(phased[m], field[which])

        @pl.when(z < 3)
        def _():
            transport(
                links, z, 2, lambda comp, at, lanes: vt[z + 1, comp, at, lanes], field.at[2]
            )
            for m in range(2):
                acc[2 * m] += dot_nt(phased[m], field[2])

        return 0

    lax.fori_loop(0, 4, plane, 0)


def edge_kernel(ints, shifts, halo, links, acc, phased, out, vt, field):
    unit = unit_matrix(128)
    for comp in range(6):
        vt[comp] = dot_nt(unit, halo[comp // 3, comp % 3])
    transport(links, 0, 2, lambda comp, at, lanes: vt[comp, at, lanes], field)
    for m in range(2):
        along = jnp.where(ints[6 + 2 * m] == 3, 0, 1)
        for o in range(2):
            t = acc[2 * m + o]
            if o == 0:
                t = t + dot_nt(phased[m], field[...])
                slot = along
            else:
                slot = 1 - along
            direction = ints[6 + 2 * m + slot] - 1
            cd = shifts[2 * (m * 3 + direction)]
            sd = shifts[2 * (m * 3 + direction) + 1]
            ar = t[0:128, 0:128] - t[128:256, 128:256]
            ai = t[0:128, 128:256] + t[128:256, 0:128]
            br = (t[256:384, 0:128] - t[384:512, 128:256]).T
            bi = (t[256:384, 128:256] + t[384:512, 0:128]).T
            out[2 * m + slot, 0] = ar - cd * br + sd * bi
            out[2 * m + slot, 1] = ai + sd * br + cd * bi


def loop_kernel(phi, tau0, tau1, tau2, tau3, out):
    lhs = jnp.concatenate([phi[0], phi[1]], axis=1)

    def slot(s, _):
        total = jnp.zeros((128, 256), F32)
        for tau in (tau0, tau1, tau2, tau3):
            for beta in range(4):
                tr = tau[s, beta, 0]
                ti = tau[s, beta, 1]
                rhs = jnp.concatenate(
                    [jnp.concatenate([tr, ti], axis=1), jnp.concatenate([-ti, tr], axis=1)], axis=0
                )
                mid = dot_nn(lhs, rhs).astype(BF)
                zr, zi = mid[:, :128], mid[:, 128:]
                rhs = jnp.concatenate(
                    [jnp.concatenate([zr, zi], axis=1), jnp.concatenate([zi, -zr], axis=1)], axis=0
                )
                left = jnp.concatenate([tr, ti], axis=0)
                total = total + lax.dot_general(
                    left, rhs, (((0,), (0,)), ((), ())), preferred_element_type=F32
                )
        out[s, 0] = total[:, :128]
        out[s, 1] = total[:, 128:]
        return 0

    lax.fori_loop(0, 4, slot, 0)


VMEM = pl.BlockSpec(memory_space=pltpu.VMEM)
SMEM = pl.BlockSpec(memory_space=pltpu.SMEM)


def call(kernel, outs, inputs, scratch, flops, moved):
    return pl.pallas_call(
        kernel,
        out_shape=outs,
        in_specs=[SMEM if x.ndim == 1 else VMEM for x in inputs],
        out_specs=jax.tree.map(lambda _: VMEM, outs),
        scratch_shapes=scratch,
        compiler_params=pltpu.CompilerParams(vmem_limit_bytes=48 * 2**20),
        cost_estimate=pl.CostEstimate(flops=flops, bytes_accessed=moved, transcendentals=0),
    )(*inputs)


def partner(value, axis, distance=1):
    n = lax.axis_size(axis)
    return lax.ppermute(value, axis, [((i + distance) % n, i) for i in range(n)])


def on_device(eigvecs, gauge_links, peramb, momenta, disp_paths, sources):
    eig = eigvecs[0]
    depth = eig.shape[2]
    lower = lax.axis_index("xl") * 2 + lax.axis_index("c")
    halo_out = eig[:, :, 0]
    halo = lax.ppermute(halo_out, GZ, [((i + 1) % 4, i) for i in range(4)])
    links = jnp.swapaxes(gauge_links[0].reshape(54, depth, LX * LY), 0, 1).astype(F32)
    ints = jnp.concatenate(
        [momenta.reshape(6), disp_paths.reshape(4), (lower * depth)[None].astype(jnp.int32)]
    )
    turn = (momenta.reshape(6) & 15).astype(F32) * (2.0 * math.pi / 16.0)
    shifts = jnp.stack([jnp.cos(turn), jnp.sin(turn)], axis=1).reshape(12)
    acc, phased = call(
        local_kernel,
        (jax.ShapeDtypeStruct((4, 512, 256), F32), jax.ShapeDtypeStruct((2, 512, 768), BF)),
        (ints, eig, links),
        [
            pltpu.VMEM((4, 6, 128, 256), F32),
            pltpu.VMEM((6, 128, 256), F32),
            pltpu.VMEM((3, 256, 768), BF),
            pltpu.VMEM((2, 256, 256), BF),
        ],
        4 * 10**9,
        5 * 10**6,
    )
    partial = call(
        edge_kernel,
        jax.ShapeDtypeStruct((4, 2, 128, 128), F32),
        (ints, shifts, halo, links[depth - 1 :], acc, phased),
        [pltpu.VMEM((6, 128, 256), F32), pltpu.VMEM((256, 768), BF)],
        5 * 10**8,
        5 * 10**6,
    )
    norm_scale = 1.0 / math.sqrt(12.0 * LX * LY * depth * 4)
    shares = lax.all_to_all(partial, GZ, 0, 0, tiled=True)
    phi = (jnp.sum(shares, axis=0) * norm_scale).astype(BF)

    chunks = lax.all_to_all(phi.reshape(32, 8, 128), YZ, 0, 0, tiled=True)
    mine = (sources & 1) == lax.axis_index("xh")
    picked = jnp.stack(
        [lax.dynamic_index_in_dim(chunks, sources[s] >> 1, 0, keepdims=False) for s in range(NSRC)]
    )
    other = lax.ppermute(picked, "xh", [(0, 1), (1, 0)])
    picked = jnp.where(mine[:, None, None], picked, other)
    spread = jnp.broadcast_to(picked[None], (32, NSRC, 8, 128))
    source_phi = lax.all_to_all(spread, YZ, 0, 0, tiled=True)
    source_phi = jnp.swapaxes(source_phi, 0, 1).reshape(NSRC, 2, 128, 128).astype(F32)

    tau = peramb[0, :, 0]
    tau, phi_held = lax.optimization_barrier((tau, phi))
    tau_far = partner(tau, "xl")
    tau_near = partner(tau, "c")
    tau_diag = partner(tau_far, "c")
    looped = call(
        loop_kernel,
        jax.ShapeDtypeStruct((NSRC, 2, 128, 128), F32),
        (phi_held, tau, tau_near, tau_far, tau_diag),
        [],
        2 * 10**9,
        5 * 10**6,
    )
    real = jnp.sum(looped * source_phi, axis=(1, 2, 3))
    imag = jnp.sum(looped[:, 1] * source_phi[:, 0] - looped[:, 0] * source_phi[:, 1], axis=(1, 2))
    pair = jnp.stack([real, imag], axis=-1) / (8.0 * 128)
    owned = jnp.arange(4, dtype=jnp.int32) == lower
    spreadout = jnp.where(owned[None, :, None], pair[:, None, :], 0.0)
    correlator = lax.psum(spreadout, GZ).reshape(NSRC, 1, 2, 2, 2)

    rows = lax.all_to_all(
        jnp.swapaxes(phi.reshape(2, 4, 32, 128), 0, 1), GZ, 0, 0, tiled=True
    )
    return rows.reshape(1, 2, 2, 2, 32, 128), correlator


def solution(mesh):
    fine = Mesh(np.asarray(mesh.devices).reshape(4, 8, 2, 2, 2), (*TA, *GZ))
    placed = (
        P(TA, None, None, GZ, None, None),
        P(TA, None, None, None, None, GZ, None),
        P(TA, None, GZ, None, None, None, None),
        P(),
        P(),
        P(),
    )
    return jax.shard_map(
        on_device,
        mesh=fine,
        in_specs=placed,
        out_specs=(P(TA, None, None, None, GZ, None), P(None, TA, None, None, None)),
        check_vma=False,
    )
```

```python
import functools
import math

import jax
import jax.numpy as jnp
import numpy as np
from jax import lax
from jax.experimental import pallas as pl
from jax.experimental.pallas import tpu as pltpu
from jax.sharding import Mesh
from jax.sharding import PartitionSpec as P

LX = 16
LY = 16
NSRC = 4
BF = jnp.bfloat16
F32 = jnp.float32
NT_DIMS = (((1,), (1,)), ((), ()))
TA = ("y", "z", "xh")
YZ = ("y", "z")
GZ = ("xl", "c")


def dot_nt(a, b):
    return lax.dot_general(a, b, NT_DIMS, preferred_element_type=F32)


def dot_nn(a, b):
    return jnp.dot(a, b, preferred_element_type=F32)


def shift_matrix(direction):
    row = lax.broadcasted_iota(jnp.int32, (256, 256), 0)
    col = lax.broadcasted_iota(jnp.int32, (256, 256), 1)
    if direction == 0:
        target = (col + LY) & 255
    else:
        target = (col & ~(LY - 1)) | ((col + 1) & (LY - 1))
    return jnp.where(row == target, 1.0, 0.0).astype(F32).astype(BF)


def unit_matrix(n):
    row = lax.broadcasted_iota(jnp.int32, (n, n), 0)
    col = lax.broadcasted_iota(jnp.int32, (n, n), 1)
    return jnp.where(row == col, 1.0, 0.0).astype(F32).astype(BF)


def transport(links, z, direction, source, target):
    for half in range(2):
        lanes = pl.ds(half * 128, 128)
        coef = [
            [
                [
                    jnp.broadcast_to(
                        links[z, pl.ds(direction * 18 + a * 6 + b * 2 + part, 1), lanes], (8, 128)
                    )
                    for part in range(2)
                ]
                for b in range(3)
            ]
            for a in range(3)
        ]

        for step in range(8):
            parts = []
            for sub in range(2):
                at = pl.ds(step * 16 + sub * 8, 8)
                vec = [[source(part * 3 + b, at, lanes) for b in range(3)] for part in range(2)]
                out = []
                for a in range(3):
                    re = im = None
                    for b in range(3):
                        ur, ui = coef[a][b]
                        tr = ur * vec[0][b] - ui * vec[1][b]
                        ti = ur * vec[1][b] + ui * vec[0][b]
                        re = tr if re is None else re + tr
                        im = ti if im is None else im + ti
                    out.append((re, im))
                parts.append(out)
            for a in range(3):
                for part in range(2):
                    block = jnp.concatenate([parts[0][a][part], parts[1][a][part]], axis=0)
                    start = part * 128 + step * 16
                    target[pl.ds(start, 16), pl.ds(a * 256 + half * 128, 128)] = block.astype(BF)


def phase_rows(ints, row, plane):
    site = lax.broadcasted_iota(jnp.int32, (8, 256), 1)
    x1 = site >> 4
    x2 = site & (LY - 1)
    steps = ints[row * 3] * x1 + ints[row * 3 + 1] * x2 + ints[row * 3 + 2] * plane
    angle = (steps & 15).astype(F32) * (2.0 * math.pi / 16.0)
    return jnp.cos(angle), jnp.sin(angle)


def phase_plane(ints, z, vt, phased):
    for m in range(2):
        cosine, sine = phase_rows(ints, m, ints[10] + z)
        for half in range(2):
            lanes = pl.ds(half * 128, 128)
            cs = cosine[:, half * 128 : half * 128 + 128]
            sn = sine[:, half * 128 : half * 128 + 128]
            cs = jnp.concatenate([cs] * 2, axis=0)
            sn = jnp.concatenate([sn] * 2, axis=0)
            for step in range(8):
                at = pl.ds(step * 16, 16)
                for a in range(3):
                    re = vt[z, a, at, lanes]
                    im = vt[z, 3 + a, at, lanes]
                    rc, rs, ic, js = re * cs, re * sn, im * cs, im * sn
                    to = pl.ds(a * 256 + half * 128, 128)
                    for block, value in enumerate((rc - js, -(rs + ic), rc + js, rs - ic)):
                        phased[m, pl.ds(block * 128 + step * 16, 16), to] = value.astype(BF)


def local_kernel(ints, eig, narrow, acc, phased, edge_links, vt, vs, field, perm, links):
    unit = unit_matrix(128)
    perm[0] = shift_matrix(0)
    perm[1] = shift_matrix(1)
    wide = narrow[...].astype(F32)
    for z in range(4):
        links[z] = wide[:, z, :]
    edge_links[0] = links[3]

    def load(z, _):
        for comp in range(6):
            vt[z, comp] = dot_nt(unit, eig[comp // 3, comp % 3, z])
        return 0
    lax.fori_loop(0, 4, load, 0)
    acc[...] = jnp.zeros_like(acc)
    which = [jnp.where(ints[6 + 2 * m] == 3, ints[7 + 2 * m], ints[6 + 2 * m]) - 1 for m in range(2)]
    def plane(z, last):
        phase_plane(ints, z, vt, phased)
        for direction in range(2):
            vs[direction] = dot_nn(vt[z].reshape(768, 256).astype(BF), perm[direction]).reshape(6, 128, 256)
        for direction in range(2):
            transport(links, z, direction, lambda comp, at, lanes: vs[direction, comp, at, lanes], field.at[direction])
        if not last:
            transport(links, z, 2, lambda comp, at, lanes: vt[z + 1, comp, at, lanes], field.at[2])
            t = dot_nt(phased[...].reshape(1024, 768), field[2])
            acc[0] += t[:512]
            acc[2] += t[512:]
        for m in range(2):
            acc[2 * m + 1] += dot_nt(phased[m], field[which[m]])
        return 0
    lax.fori_loop(0, 3, lambda z, _: plane(z, False), 0)
    plane(3, True)


def edge_kernel(ints, halo, links, acc, phased, tau, keep, send, rest, vt, field):
    unit = unit_matrix(128)
    for comp in range(6):
        vt[comp] = dot_nt(unit, halo[comp // 3, comp % 3])
    transport(links, 0, 2, lambda comp, at, lanes: vt[comp, at, lanes], field)
    rest[...] = tau[1:4]
    core = ints[11] & 1
    edge = dot_nt(phased[...].reshape(1024, 768), field[...])
    for m in range(2):
        along = jnp.where(ints[6 + 2 * m] == 3, 0, 1)
        for o in range(2):
            t = acc[2 * m + o]
            if o == 0:
                t = t + edge[512 * m : 512 * m + 512]
                slot = along
            else:
                slot = 1 - along
            direction = ints[6 + 2 * m + slot] - 1
            turn = jnp.full((8, 128), ints[3 * m + direction] & 15, jnp.int32).astype(F32)
            turn = turn * (2.0 * math.pi / 16.0)
            cd = jnp.cos(turn)[:1]
            sd = jnp.sin(turn)[:1]
            ar = t[0:128, 0:128] - t[128:256, 128:256]
            ai = t[0:128, 128:256] + t[128:256, 0:128]
            br = (t[256:384, 0:128] - t[384:512, 128:256]).T
            bi = (t[256:384, 128:256] + t[384:512, 0:128]).T
            re = ar - cd * br + sd * bi
            im = ai + sd * br + cd * bi

            def store(ref, m=m, re=re, im=im):
                ref[m, 0] = re
                ref[m, 1] = im

            pl.when(slot == core)(functools.partial(store, keep))
            pl.when(slot != core)(functools.partial(store, send))


def pieces_kernel(eig, tau, lowest, head, sems):
    moves = [(eig.at[part, a, 0], lowest.at[part, a]) for part in range(2) for a in range(3)]
    moves.append((tau.at[pl.ds(0, 1)], head))
    copies = [pltpu.make_async_copy(*move, sems.at[n]) for n, move in enumerate(moves)]
    for copy in copies:
        copy.start()
    for copy in copies:
        copy.wait()


def table_kernel(ints, pair0, pair1, pair2, pair3, table):
    lane = lax.broadcasted_iota(jnp.int32, (8, 128), 1)
    total = jnp.zeros((8, 128), F32)
    for d, got in enumerate((pair0, pair1, pair2, pair3)):
        total = jnp.where(lane == ((ints[11] + 4 - d) & 3), got[...], total)
    table[...] = total


def half_kernel(ints, keep, got, mine, other):
    chip = ints[11] >> 1
    mine[...] = keep[chip] + got[chip]
    other[...] = (keep[1 - chip] + got[1 - chip]).astype(BF)


def phi_kernel(ints, mine, got, phi, row0, row1, row2, row3):
    phi[...] = ((mine[...] + got[...].astype(F32)) * (1.0 / math.sqrt(12.0 * LX * LY * 16))).astype(BF)
    for d, out in enumerate((row0, row1, row2, row3)):
        rows = pl.ds(pl.multiple_of(((ints[11] + d) & 3) * 32, 32), 32)
        for part in range(2):
            out[part] = phi[part, rows, :]


def pick_kernel(sources, chunks, out):
    for s in range(NSRC):
        out[s] = chunks[sources[s] >> 1]


def spread_kernel(ints, sources, mine, other, out):
    for s in range(NSRC):
        value = jnp.where((sources[s] & 1) == ints[12], mine[s], other[s])
        for place in range(32):
            out[place, s] = value


def loop_kernel(phi, whole, *refs, start):
    first = jnp.concatenate(
        [
            jnp.concatenate([phi[0], phi[1]], axis=1),
            jnp.concatenate([phi[1], -phi[0]], axis=1),
        ],
        axis=0,
    )
    out = refs[-1]
    for s in range(NSRC):
        piece, at = (0, 0) if s == 0 else (1, s - 1)
        taus = [(ref, at) for ref in refs[piece:-1:2]]
        if start:
            total = jnp.zeros((128, 256), F32)
            taus.append((whole, s))
        else:
            total = jnp.concatenate([whole[s, 0], whole[s, 1]], axis=1)
        for tau, at in taus:
            pairs = [(tau[at, beta, 0], tau[at, beta, 1]) for beta in range(4)]
            left = jnp.concatenate([jnp.concatenate(pair, axis=0) for pair in pairs], axis=1)
            mid = lax.dot_general(
                left, first, (((0,), (0,)), ((), ())), preferred_element_type=F32
            ).astype(BF)
            mid = jnp.concatenate([mid[beta * 128 : beta * 128 + 128] for beta in range(4)], axis=1)
            second = jnp.concatenate(
                [
                    jnp.concatenate(row, axis=1)
                    for tr, ti in pairs
                    for row in ((tr, ti), (-ti, tr))
                ],
                axis=0,
            )
            total = total + dot_nn(mid, second)
        out[s, 0] = total[:, :128]
        out[s, 1] = total[:, 128:]


def close_kernel(ints, looped, spread, row0, row1, row2, row3, rows, pair):
    for d, got in enumerate((row0, row1, row2, row3)):
        rows[(ints[11] + 4 - d) & 3] = got[...]
    for s in range(NSRC):
        src_re = spread[0:16, s].astype(F32).reshape(128, 128)
        src_im = spread[16:32, s].astype(F32).reshape(128, 128)
        yr, yi = looped[s, 0], looped[s, 1]
        re = jnp.sum(yr * src_re + yi * src_im) * (1.0 / (8.0 * 128))
        im = jnp.sum(yi * src_re - yr * src_im) * (1.0 / (8.0 * 128))
        pair[2 * s : 2 * s + 1, :] = jnp.full((1, 128), re, F32)
        pair[2 * s + 1 : 2 * s + 2, :] = jnp.full((1, 128), im, F32)


VMEM = pl.BlockSpec(memory_space=pltpu.VMEM)
SMEM = pl.BlockSpec(memory_space=pltpu.SMEM)


def call(kernel, outs, inputs, scratch, flops, moved):
    return pl.pallas_call(
        kernel,
        out_shape=outs,
        in_specs=[SMEM if x.ndim == 1 else VMEM for x in inputs],
        out_specs=jax.tree.map(lambda _: VMEM, outs),
        scratch_shapes=scratch,
        compiler_params=pltpu.CompilerParams(vmem_limit_bytes=40 * 2**20),
        cost_estimate=pl.CostEstimate(flops=flops, bytes_accessed=moved, transcendentals=0),
    )(*inputs)


def partner(value, axis, distance=1):
    n = math.prod(lax.axis_size(name) for name in ([axis] if isinstance(axis, str) else axis))
    return lax.ppermute(value, axis, [((i + distance) % n, i) for i in range(n)])


def shaped(*shape, dtype=F32):
    return jax.ShapeDtypeStruct(shape, dtype)


def on_device(eigvecs, gauge_links, peramb, momenta, disp_paths, sources):
    eig = eigvecs[0]
    depth = eig.shape[2]
    own = lax.axis_index("xl") * 2 + lax.axis_index("c")
    tau = peramb[0, :, 0]
    piece = [shaped(n, *tau.shape[1:], dtype=BF) for n in (1, 3)]
    lowest, head = pl.pallas_call(
        pieces_kernel,
        out_shape=(shaped(2, 3, 256, 128, dtype=BF), piece[0]),
        in_specs=[pl.BlockSpec(memory_space=pl.ANY)] * 2,
        out_specs=(VMEM,) * 2,
        scratch_shapes=[pltpu.SemaphoreType.DMA((7,))],
    )(eig, tau)
    halo = partner(lowest, GZ)
    near = partner(tau, "c")
    far = [partner(head, "xl")]
    links = gauge_links[0].reshape(54, depth, LX * LY)
    ints = jnp.concatenate(
        [
            momenta.reshape(6),
            disp_paths.reshape(4),
            jnp.stack([own * depth, own, lax.axis_index("xh")]).astype(jnp.int32),
        ]
    )
    acc, phased, edge_links = call(
        local_kernel,
        (shaped(4, 512, 256), shaped(2, 512, 768, dtype=BF), shaped(1, 54, 256)),
        (ints, eig, links),
        [
            pltpu.VMEM((4, 6, 128, 256), F32),
            pltpu.VMEM((2, 6, 128, 256), F32),
            pltpu.VMEM((3, 256, 768), BF),
            pltpu.VMEM((2, 256, 256), BF),
            pltpu.VMEM((depth, 54, 256), F32),
        ],
        4 * 10**9,
        5 * 10**6,
    )
    far[0], acc = lax.optimization_barrier((far[0], acc))
    keep, send, rest = call(
        edge_kernel,
        (shaped(2, 2, 128, 128), shaped(2, 2, 128, 128), piece[1]),
        (ints, halo, edge_links, acc, phased, tau),
        [pltpu.VMEM((6, 128, 256), F32), pltpu.VMEM((256, 768), BF)],
        5 * 10**8,
        5 * 10**6,
    )
    whole = shaped(2, 128, 128)
    mine, other = call(half_kernel, (whole, shaped(2, 128, 128, dtype=BF)), (ints, keep, partner(send, "c")), [], 10**5, 10**6)
    arrived = partner(other, "xl")
    last, arrived = lax.optimization_barrier((rest, arrived))
    far.append(partner(last, "xl"))
    block = shaped(2, 32, 128, dtype=BF)
    phi, *rows = call(
        phi_kernel,
        (shaped(2, 128, 128, dtype=BF), block, block, block, block),
        (ints, mine, arrived),
        [],
        10**5,
        10**6,
    )

    chunks = lax.all_to_all(phi.reshape(32, 8, 128), YZ, 0, 0, tiled=True)
    four = shaped(NSRC, 8, 128, dtype=BF)
    picked = call(pick_kernel, four, (sources, chunks), [], 10**4, 10**5)
    crossed = partner(picked, "xh")
    phi, _, far, rows = lax.optimization_barrier((phi, picked, far, rows))
    diagonal = [partner(piece, "c") for piece in far]
    rows = rows[:1] + [partner(row, GZ, -d) for d, row in enumerate(rows) if d]
    looped = shaped(NSRC, 2, 128, 128)
    partly = call(
        functools.partial(loop_kernel, start=True),
        looped,
        (phi, near, head, rest, *far),
        [],
        15 * 10**8,
        4 * 10**6,
    )
    looped = call(
        functools.partial(loop_kernel, start=False),
        looped,
        (phi, partly, *diagonal),
        [],
        5 * 10**8,
        2 * 10**6,
    )
    looped, crossed, *rows = lax.optimization_barrier((looped, crossed, *rows))
    spread = call(
        spread_kernel,
        shaped(32, NSRC, 8, 128, dtype=BF),
        (ints, sources, picked, crossed),
        [],
        10**4,
        10**5,
    )
    spread = lax.all_to_all(spread, YZ, 0, 0, tiled=True)
    rows, pair = call(
        close_kernel,
        (shaped(4, 2, 32, 128, dtype=BF), shaped(8, 128)),
        (ints, looped, spread, *rows),
        [],
        10**5,
        10**6,
    )
    pairs = [pair] + [partner(pair, GZ, -d) for d in range(1, 4)]
    table = call(table_kernel, shaped(8, 128), (ints, *pairs), [], 10**3, 10**4)
    correlator = jnp.swapaxes(table[:, :4].reshape(NSRC, 2, 4), 1, 2)
    return rows.reshape(1, 2, 2, 2, 32, 128), correlator.reshape(NSRC, 1, 2, 2, 2)


def solution(mesh):
    fine = Mesh(np.asarray(mesh.devices).reshape(4, 8, 2, 2, 2), (*TA, *GZ))
    placed = (
        P(TA, None, None, GZ, None, None),
        P(TA, None, None, None, None, GZ, None),
        P(TA, None, GZ, None, None, None, None),
        P(),
        P(),
        P(),
    )
    return jax.shard_map(
        on_device,
        mesh=fine,
        in_specs=placed,
        out_specs=(P(TA, None, None, None, GZ, None), P(None, TA, None, None, None)),
        check_vma=False,
    )
```

```python
import functools
import math

import jax
import jax.numpy as jnp
import numpy as np
from jax import lax
from jax.experimental import pallas as pl
from jax.experimental.pallas import tpu as pltpu
from jax.sharding import Mesh
from jax.sharding import PartitionSpec as P

LX = 16
LY = 16
NSRC = 4
BF = jnp.bfloat16
F32 = jnp.float32
NT_DIMS = (((1,), (1,)), ((), ()))
TA = ("y", "z", "xh")
YZ = ("y", "z")
GZ = ("xl", "c")


def dot_nt(a, b):
    return lax.dot_general(a, b, NT_DIMS, preferred_element_type=F32)


def dot_nn(a, b):
    return jnp.dot(a, b, preferred_element_type=F32)


def shift_matrix(direction):
    row = lax.broadcasted_iota(jnp.int32, (256, 256), 0)
    col = lax.broadcasted_iota(jnp.int32, (256, 256), 1)
    if direction == 0:
        target = (col + LY) & 255
    else:
        target = (col & ~(LY - 1)) | ((col + 1) & (LY - 1))
    return jnp.where(row == target, 1.0, 0.0).astype(F32).astype(BF)


def unit_matrix(n):
    row = lax.broadcasted_iota(jnp.int32, (n, n), 0)
    col = lax.broadcasted_iota(jnp.int32, (n, n), 1)
    return jnp.where(row == col, 1.0, 0.0).astype(F32).astype(BF)


def transport(links, z, direction, source, target):
    for half in range(2):
        lanes = pl.ds(half * 128, 128)
        coef = [
            [
                [
                    jnp.broadcast_to(
                        links[z, pl.ds(direction * 18 + a * 6 + b * 2 + part, 1), lanes], (8, 128)
                    )
                    for part in range(2)
                ]
                for b in range(3)
            ]
            for a in range(3)
        ]

        for step in range(8):
            parts = []
            for sub in range(2):
                at = pl.ds(step * 16 + sub * 8, 8)
                vec = [[source(part * 3 + b, at, lanes) for b in range(3)] for part in range(2)]
                out = []
                for a in range(3):
                    re = im = None
                    for b in range(3):
                        ur, ui = coef[a][b]
                        tr = ur * vec[0][b] - ui * vec[1][b]
                        ti = ur * vec[1][b] + ui * vec[0][b]
                        re = tr if re is None else re + tr
                        im = ti if im is None else im + ti
                    out.append((re, im))
                parts.append(out)
            for a in range(3):
                for part in range(2):
                    block = jnp.concatenate([parts[0][a][part], parts[1][a][part]], axis=0)
                    start = part * 128 + step * 16
                    target[pl.ds(start, 16), pl.ds(a * 256 + half * 128, 128)] = block.astype(BF)


def phase_rows(ints, row, plane):
    site = lax.broadcasted_iota(jnp.int32, (8, 256), 1)
    x1 = site >> 4
    x2 = site & (LY - 1)
    steps = ints[row * 3] * x1 + ints[row * 3 + 1] * x2 + ints[row * 3 + 2] * plane
    angle = (steps & 15).astype(F32) * (2.0 * math.pi / 16.0)
    return jnp.cos(angle), jnp.sin(angle)


def phase_plane(ints, z, vt, phased):
    for m in range(2):
        cosine, sine = phase_rows(ints, m, ints[10] + z)
        for half in range(2):
            lanes = pl.ds(half * 128, 128)
            cs = cosine[:, half * 128 : half * 128 + 128]
            sn = sine[:, half * 128 : half * 128 + 128]
            cs = jnp.concatenate([cs] * 2, axis=0)
            sn = jnp.concatenate([sn] * 2, axis=0)
            for step in range(8):
                at = pl.ds(step * 16, 16)
                for a in range(3):
                    re = vt[z, a, at, lanes]
                    im = vt[z, 3 + a, at, lanes]
                    rc, rs, ic, js = re * cs, re * sn, im * cs, im * sn
                    to = pl.ds(a * 256 + half * 128, 128)
                    for block, value in enumerate((rc - js, -(rs + ic), rc + js, rs - ic)):
                        phased[m, pl.ds(block * 128 + step * 16, 16), to] = value.astype(BF)


def local_kernel(ints, eig, narrow, acc, phased, edge_links, vt, vs, field, perm, links):
    unit = unit_matrix(128)
    perm[0] = shift_matrix(0)
    perm[1] = shift_matrix(1)
    wide = narrow[...].astype(F32)
    for z in range(4):
        links[z] = wide[:, z, :]
    edge_links[0] = links[3]

    def load(z, _):
        for comp in range(6):
            vt[z, comp] = dot_nt(unit, eig[comp // 3, comp % 3, z])
        return 0
    lax.fori_loop(0, 4, load, 0)
    acc[...] = jnp.zeros_like(acc)
    which = [jnp.where(ints[6 + 2 * m] == 3, ints[7 + 2 * m], ints[6 + 2 * m]) - 1 for m in range(2)]
    def plane(z, last):
        phase_plane(ints, z, vt, phased)
        for direction in range(2):
            vs[direction] = dot_nn(vt[z].reshape(768, 256).astype(BF), perm[direction]).reshape(6, 128, 256)
        for direction in range(2):
            transport(links, z, direction, lambda comp, at, lanes: vs[direction, comp, at, lanes], field.at[direction])
        if not last:
            transport(links, z, 2, lambda comp, at, lanes: vt[z + 1, comp, at, lanes], field.at[2])
            t = dot_nt(phased[...].reshape(1024, 768), field[2])
            acc[0] += t[:512]
            acc[2] += t[512:]
        for m in range(2):
            acc[2 * m + 1] += dot_nt(phased[m], field[which[m]])
        return 0
    lax.fori_loop(0, 3, lambda z, _: plane(z, False), 0)
    plane(3, True)


def edge_kernel(ints, halo, links, acc, phased, tau, keep, send, rest, vt, field):
    unit = unit_matrix(128)
    for comp in range(6):
        vt[comp] = dot_nt(unit, halo[comp // 3, comp % 3])
    transport(links, links.shape[0] - 1, 2, lambda comp, at, lanes: vt[comp, at, lanes], field)
    rest[...] = tau[1:4]
    core = ints[11] & 1
    edge = dot_nt(phased[...].reshape(1024, 768), field[...])
    for m in range(2):
        along = jnp.where(ints[6 + 2 * m] == 3, 0, 1)
        for o in range(2):
            t = acc[2 * m + o]
            if o == 0:
                t = t + edge[512 * m : 512 * m + 512]
                slot = along
            else:
                slot = 1 - along
            direction = ints[6 + 2 * m + slot] - 1
            turn = jnp.full((8, 128), ints[3 * m + direction] & 15, jnp.int32).astype(F32)
            turn = turn * (2.0 * math.pi / 16.0)
            cd = jnp.cos(turn)[:1]
            sd = jnp.sin(turn)[:1]
            ar = t[0:128, 0:128] - t[128:256, 128:256]
            ai = t[0:128, 128:256] + t[128:256, 0:128]
            br = (t[256:384, 0:128] - t[384:512, 128:256]).T
            bi = (t[256:384, 128:256] + t[384:512, 0:128]).T
            re = ar - cd * br + sd * bi
            im = ai + sd * br + cd * bi

            def store(ref, m=m, re=re, im=im):
                ref[m, 0] = re
                ref[m, 1] = im

            pl.when(slot == core)(functools.partial(store, keep))
            pl.when(slot != core)(functools.partial(store, send))


def pieces_kernel(eig, tau, lowest, head, sems):
    moves = [(eig.at[part, a, 0], lowest.at[part, a]) for part in range(2) for a in range(3)]
    moves.append((tau.at[pl.ds(0, 1)], head))
    copies = [pltpu.make_async_copy(*move, sems.at[n]) for n, move in enumerate(moves)]
    for copy in copies:
        copy.start()
    for copy in copies:
        copy.wait()


def final_kernel(ints, pair, phi, got1, got2, got3, rows, correlator):
    own = ints[11]
    mine = pl.ds(pl.multiple_of(own * 32, 32), 32)
    for part in range(2):
        rows[own, part] = phi[part, mine, :]
    sums = [jnp.sum(pair[...], axis=1, keepdims=True)]
    for d, got in enumerate((got1, got2, got3), 1):
        rows[(own + 4 - d) & 3] = got[8:72].astype(BF).reshape(2, 32, 128)
        sums.append(jnp.sum(got[0:8], axis=1, keepdims=True))
    sub = lax.broadcasted_iota(jnp.int32, (2, NSRC), 0)
    lane = lax.broadcasted_iota(jnp.int32, (2, NSRC), 1)
    for m in range(2):
        for k in range(2):
            total = jnp.zeros((8, 1), F32)
            for d, value in enumerate(sums):
                total = jnp.where(((own + 4 - d) & 3) == 2 * m + k, value, total)
            block = jnp.zeros((2, NSRC), F32)
            for s in range(NSRC):
                for part in range(2):
                    value = jnp.broadcast_to(total[2 * s + part : 2 * s + part + 1], (2, NSRC))
                    block = jnp.where((sub == part) & (lane == s), value, block)
            correlator[m, k] = block


def half_kernel(ints, keep, got, mine, other):
    chip = ints[11] >> 1
    mine[...] = keep[chip] + got[chip]
    other[...] = (keep[1 - chip] + got[1 - chip]).astype(BF)


def phi_kernel(mine, got, phi):
    total = mine[...] + got[...].astype(F32)
    phi[...] = (total * (1.0 / math.sqrt(12.0 * LX * LY * 16))).astype(BF)


def pick_kernel(sources, chunks, out):
    for s in range(NSRC):
        out[s] = chunks[sources[s] >> 1]


def spread_kernel(ints, sources, mine, other, out):
    for s in range(NSRC):
        value = jnp.where((sources[s] & 1) == ints[12], mine[s], other[s])
        for place in range(32):
            out[place, s] = value


def loop_kernel(phi, whole, *refs, start):
    first = jnp.concatenate(
        [
            jnp.concatenate([phi[0], phi[1]], axis=1),
            jnp.concatenate([phi[1], -phi[0]], axis=1),
        ],
        axis=0,
    )
    out = refs[-1]
    for s in range(NSRC):
        piece, at = (0, 0) if s == 0 else (1, s - 1)
        taus = [(ref, at) for ref in refs[piece:-1:2]]
        if start:
            total = jnp.zeros((128, 256), F32)
            taus.append((whole, s))
        else:
            total = jnp.concatenate([whole[s, 0], whole[s, 1]], axis=1)
        for tau, at in taus:
            pairs = [(tau[at, beta, 0], tau[at, beta, 1]) for beta in range(4)]
            left = jnp.concatenate([jnp.concatenate(pair, axis=0) for pair in pairs], axis=1)
            mid = lax.dot_general(
                left, first, (((0,), (0,)), ((), ())), preferred_element_type=F32
            ).astype(BF)
            mid = jnp.concatenate([mid[beta * 128 : beta * 128 + 128] for beta in range(4)], axis=1)
            second = jnp.concatenate(
                [
                    jnp.concatenate(row, axis=1)
                    for tr, ti in pairs
                    for row in ((tr, ti), (-ti, tr))
                ],
                axis=0,
            )
            total = total + dot_nn(mid, second)
        out[s, 0] = total[:, :128]
        out[s, 1] = total[:, 128:]


def close_kernel(ints, looped, spread, phi, pair, send1, send2, send3):
    for s in range(NSRC):
        src_re = spread[0:16, s].astype(F32).reshape(128, 128)
        src_im = spread[16:32, s].astype(F32).reshape(128, 128)
        yr, yi = looped[s, 0], looped[s, 1]
        re = jnp.sum(yr * src_re + yi * src_im, axis=0, keepdims=True)
        im = jnp.sum(yi * src_re - yr * src_im, axis=0, keepdims=True)
        pair[2 * s : 2 * s + 1, :] = re * (1.0 / (8.0 * 128))
        pair[2 * s + 1 : 2 * s + 2, :] = im * (1.0 / (8.0 * 128))
    for d, send in enumerate((send1, send2, send3), 1):
        send[0:8] = pair[...]
        rows = pl.ds(pl.multiple_of(((ints[11] + d) & 3) * 32, 32), 32)
        for part in range(2):
            send[8 + 32 * part : 40 + 32 * part] = phi[part, rows, :].astype(F32)


VMEM = pl.BlockSpec(memory_space=pltpu.VMEM)
SMEM = pl.BlockSpec(memory_space=pltpu.SMEM)


def call(kernel, outs, inputs, scratch, flops, moved):
    return pl.pallas_call(
        kernel,
        out_shape=outs,
        in_specs=[SMEM if x.ndim == 1 else VMEM for x in inputs],
        out_specs=jax.tree.map(lambda _: VMEM, outs),
        scratch_shapes=scratch,
        compiler_params=pltpu.CompilerParams(vmem_limit_bytes=40 * 2**20),
        cost_estimate=pl.CostEstimate(flops=flops, bytes_accessed=moved, transcendentals=0),
    )(*inputs)


def partner(value, axis, distance=1):
    n = math.prod(lax.axis_size(name) for name in ([axis] if isinstance(axis, str) else axis))
    return lax.ppermute(value, axis, [((i + distance) % n, i) for i in range(n)])


def shaped(*shape, dtype=F32):
    return jax.ShapeDtypeStruct(shape, dtype)


def on_device(eigvecs, gauge_links, peramb, momenta, disp_paths, sources):
    eig = eigvecs[0]
    depth = eig.shape[2]
    own = lax.axis_index("xl") * 2 + lax.axis_index("c")
    tau = peramb[0, :, 0]
    piece = [shaped(n, *tau.shape[1:], dtype=BF) for n in (1, 3)]
    links = gauge_links[0].reshape(54, depth, LX * LY)
    lowest, head = pl.pallas_call(
        pieces_kernel,
        out_shape=(shaped(2, 3, 256, 128, dtype=BF), piece[0]),
        in_specs=[pl.BlockSpec(memory_space=pl.ANY)] * 2,
        out_specs=(VMEM,) * 2,
        scratch_shapes=[pltpu.SemaphoreType.DMA((7,))],
    )(eig, tau)
    halo = partner(lowest, GZ)
    near = partner(tau, "c")
    far = [partner(head, "xl")]
    ints = jnp.concatenate(
        [
            momenta.reshape(6),
            disp_paths.reshape(4),
            jnp.stack([own * depth, own, lax.axis_index("xh")]).astype(jnp.int32),
        ]
    )
    acc, phased, edge_links = call(
        local_kernel,
        (shaped(4, 512, 256), shaped(2, 512, 768, dtype=BF), shaped(1, 54, 256)),
        (ints, eig, links),
        [
            pltpu.VMEM((4, 6, 128, 256), F32),
            pltpu.VMEM((2, 6, 128, 256), F32),
            pltpu.VMEM((3, 256, 768), BF),
            pltpu.VMEM((2, 256, 256), BF),
            pltpu.VMEM((depth, 54, 256), F32),
        ],
        4 * 10**9,
        5 * 10**6,
    )
    far[0], acc = lax.optimization_barrier((far[0], acc))
    keep, send, rest = call(
        edge_kernel,
        (shaped(2, 2, 128, 128), shaped(2, 2, 128, 128), piece[1]),
        (ints, halo, edge_links, acc, phased, tau),
        [pltpu.VMEM((6, 128, 256), F32), pltpu.VMEM((256, 768), BF)],
        5 * 10**8,
        5 * 10**6,
    )
    whole = shaped(2, 128, 128)
    mine, other = call(half_kernel, (whole, shaped(2, 128, 128, dtype=BF)), (ints, keep, partner(send, "c")), [], 10**5, 10**6)
    arrived = partner(other, "xl")
    last, arrived = lax.optimization_barrier((rest, arrived))
    far.append(partner(last, "xl"))
    phi = call(phi_kernel, shaped(2, 128, 128, dtype=BF), (mine, arrived), [], 10**5, 10**6)

    chunks = lax.all_to_all(phi.reshape(32, 8, 128), YZ, 0, 0, tiled=True)
    four = shaped(NSRC, 8, 128, dtype=BF)
    picked = call(pick_kernel, four, (sources, chunks), [], 10**4, 10**5)
    crossed = partner(picked, "xh")
    phi, _, far = lax.optimization_barrier((phi, picked, far))
    diagonal = [partner(piece, "c") for piece in far]
    looped = shaped(NSRC, 2, 128, 128)
    partly = call(
        functools.partial(loop_kernel, start=True),
        looped,
        (phi, near, head, rest, *far),
        [],
        15 * 10**8,
        4 * 10**6,
    )
    looped = call(
        functools.partial(loop_kernel, start=False),
        looped,
        (phi, partly, *diagonal),
        [],
        5 * 10**8,
        2 * 10**6,
    )
    looped, crossed = lax.optimization_barrier((looped, crossed))
    spread = call(
        spread_kernel,
        shaped(32, NSRC, 8, 128, dtype=BF),
        (ints, sources, picked, crossed),
        [],
        10**4,
        10**5,
    )
    spread = lax.all_to_all(spread, YZ, 0, 0, tiled=True)
    pair, *sends = call(
        close_kernel,
        (shaped(8, 128), *[shaped(72, 128)] * 3),
        (ints, looped, spread, phi),
        [],
        10**5,
        10**6,
    )
    rows, correlator = call(
        final_kernel,
        (shaped(4, 2, 32, 128, dtype=BF), shaped(2, 2, 2, NSRC)),
        (ints, pair, phi, *[partner(send, GZ, -d) for d, send in enumerate(sends, 1)]),
        [],
        10**5,
        10**6,
    )
    correlator = jnp.transpose(correlator, (3, 0, 1, 2))[:, None]
    return rows.reshape(1, 2, 2, 2, 32, 128), correlator


def solution(mesh):
    fine = Mesh(np.asarray(mesh.devices).reshape(4, 8, 2, 2, 2), (*TA, *GZ))
    placed = (
        P(TA, None, None, GZ, None, None),
        P(TA, None, None, None, None, GZ, None),
        P(TA, None, GZ, None, None, None, None),
        P(),
        P(),
        P(),
    )
    return jax.shard_map(
        on_device,
        mesh=fine,
        in_specs=placed,
        out_specs=(P(TA, None, None, None, GZ, None), P(None, TA, None, None, None)),
        check_vma=False,
    )
```

```python
import functools
import math

import jax
import jax.numpy as jnp
import numpy as np
from jax import lax
from jax.experimental import pallas as pl
from jax.experimental.pallas import tpu as pltpu
from jax.sharding import Mesh
from jax.sharding import PartitionSpec as P

LX = 16
LY = 16
NSRC = 4
BF = jnp.bfloat16
F32 = jnp.float32
NT_DIMS = (((1,), (1,)), ((), ()))
TA = ("y", "z", "xh")
YZ = ("y", "z")
GZ = ("xl", "c")


def dot_nt(a, b):
    return lax.dot_general(a, b, NT_DIMS, preferred_element_type=F32)


def dot_nn(a, b):
    return jnp.dot(a, b, preferred_element_type=F32)


def shift_matrix(direction):
    row = lax.broadcasted_iota(jnp.int32, (256, 256), 0)
    col = lax.broadcasted_iota(jnp.int32, (256, 256), 1)
    if direction == 0:
        target = (col + LY) & 255
    else:
        target = (col & ~(LY - 1)) | ((col + 1) & (LY - 1))
    return jnp.where(row == target, 1.0, 0.0).astype(F32).astype(BF)


def unit_matrix(n):
    row = lax.broadcasted_iota(jnp.int32, (n, n), 0)
    col = lax.broadcasted_iota(jnp.int32, (n, n), 1)
    return jnp.where(row == col, 1.0, 0.0).astype(F32).astype(BF)


def transport(links, z, direction, source, target):
    for half in range(2):
        lanes = pl.ds(half * 128, 128)
        coef = [
            [
                [
                    jnp.broadcast_to(
                        links[z, pl.ds(direction * 18 + a * 6 + b * 2 + part, 1), lanes], (8, 128)
                    )
                    for part in range(2)
                ]
                for b in range(3)
            ]
            for a in range(3)
        ]

        for step in range(8):
            parts = []
            for sub in range(2):
                at = pl.ds(step * 16 + sub * 8, 8)
                vec = [[source(part * 3 + b, at, lanes) for b in range(3)] for part in range(2)]
                out = []
                for a in range(3):
                    re = im = None
                    for b in range(3):
                        ur, ui = coef[a][b]
                        tr = ur * vec[0][b] - ui * vec[1][b]
                        ti = ur * vec[1][b] + ui * vec[0][b]
                        re = tr if re is None else re + tr
                        im = ti if im is None else im + ti
                    out.append((re, im))
                parts.append(out)
            for a in range(3):
                for part in range(2):
                    block = jnp.concatenate([parts[0][a][part], parts[1][a][part]], axis=0)
                    start = part * 128 + step * 16
                    target[pl.ds(start, 16), pl.ds(a * 256 + half * 128, 128)] = block.astype(BF)


def phase_rows(ints, row, plane):
    site = lax.broadcasted_iota(jnp.int32, (8, 256), 1)
    x1 = site >> 4
    x2 = site & (LY - 1)
    steps = ints[row * 3] * x1 + ints[row * 3 + 1] * x2 + ints[row * 3 + 2] * plane
    angle = (steps & 15).astype(F32) * (2.0 * math.pi / 16.0)
    return jnp.cos(angle), jnp.sin(angle)


def phase_plane(ints, z, vt, phased):
    for m in range(2):
        cosine, sine = phase_rows(ints, m, ints[10] + z)
        for half in range(2):
            lanes = pl.ds(half * 128, 128)
            cs = cosine[:, half * 128 : half * 128 + 128]
            sn = sine[:, half * 128 : half * 128 + 128]
            cs = jnp.concatenate([cs] * 2, axis=0)
            sn = jnp.concatenate([sn] * 2, axis=0)
            for step in range(8):
                at = pl.ds(step * 16, 16)
                for a in range(3):
                    re = vt[z, a, at, lanes]
                    im = vt[z, 3 + a, at, lanes]
                    rc, rs, ic, js = re * cs, re * sn, im * cs, im * sn
                    to = pl.ds(a * 256 + half * 128, 128)
                    for block, value in enumerate((rc - js, -(rs + ic), rc + js, rs - ic)):
                        phased[m, pl.ds(block * 128 + step * 16, 16), to] = value.astype(BF)


def local_kernel(ints, eig, narrow, acc, phased, edge_links, vt, vs, field, perm, links):
    unit = unit_matrix(128)
    perm[0] = shift_matrix(0)
    perm[1] = shift_matrix(1)
    wide = narrow[...].astype(F32)
    for z in range(4):
        links[z] = wide[:, z, :]
    edge_links[0] = links[3]

    def load(z, _):
        for comp in range(6):
            vt[z, comp] = dot_nt(unit, eig[comp // 3, comp % 3, z])
        return 0
    lax.fori_loop(0, 4, load, 0)
    acc[...] = jnp.zeros_like(acc)
    which = [jnp.where(ints[6 + 2 * m] == 3, ints[7 + 2 * m], ints[6 + 2 * m]) - 1 for m in range(2)]
    def plane(z, last):
        phase_plane(ints, z, vt, phased)
        for direction in range(2):
            vs[direction] = dot_nn(vt[z].reshape(768, 256).astype(BF), perm[direction]).reshape(6, 128, 256)
        for direction in range(2):
            transport(links, z, direction, lambda comp, at, lanes: vs[direction, comp, at, lanes], field.at[direction])
        if not last:
            transport(links, z, 2, lambda comp, at, lanes: vt[z + 1, comp, at, lanes], field.at[2])
            t = dot_nt(phased[...].reshape(1024, 768), field[2])
            acc[0] += t[:512]
            acc[2] += t[512:]
        for m in range(2):
            acc[2 * m + 1] += dot_nt(phased[m], field[which[m]])
        return 0
    lax.fori_loop(0, 3, lambda z, _: plane(z, False), 0)
    plane(3, True)


def edge_kernel(ints, halo, links, acc, phased, tau, keep, send, rest, vt, field):
    unit = unit_matrix(128)
    for comp in range(6):
        vt[comp] = dot_nt(unit, halo[comp // 3, comp % 3])
    transport(links, links.shape[0] - 1, 2, lambda comp, at, lanes: vt[comp, at, lanes], field)
    rest[...] = tau[1:4]
    core = ints[11] & 1
    edge = dot_nt(phased[...].reshape(1024, 768), field[...])
    for m in range(2):
        along = jnp.where(ints[6 + 2 * m] == 3, 0, 1)
        for o in range(2):
            t = acc[2 * m + o]
            if o == 0:
                t = t + edge[512 * m : 512 * m + 512]
                slot = along
            else:
                slot = 1 - along
            direction = ints[6 + 2 * m + slot] - 1
            turn = jnp.full((8, 128), ints[3 * m + direction] & 15, jnp.int32).astype(F32)
            turn = turn * (2.0 * math.pi / 16.0)
            cd = jnp.cos(turn)[:1]
            sd = jnp.sin(turn)[:1]
            ar = t[0:128, 0:128] - t[128:256, 128:256]
            ai = t[0:128, 128:256] + t[128:256, 0:128]
            br = (t[256:384, 0:128] - t[384:512, 128:256]).T
            bi = (t[256:384, 128:256] + t[384:512, 0:128]).T
            re = ar - cd * br + sd * bi
            im = ai + sd * br + cd * bi

            def store(ref, m=m, re=re, im=im):
                ref[m, 0] = re
                ref[m, 1] = im

            pl.when(slot == core)(functools.partial(store, keep))
            pl.when(slot != core)(functools.partial(store, send))


def pieces_kernel(eig, tau, lowest, head, sems):
    moves = [(eig.at[part, a, 0], lowest.at[part, a]) for part in range(2) for a in range(3)]
    moves.append((tau.at[pl.ds(0, 1)], head))
    copies = [pltpu.make_async_copy(*move, sems.at[n]) for n, move in enumerate(moves)]
    for copy in copies:
        copy.start()
    for copy in copies:
        copy.wait()


def final_kernel(ints, pair, phi, got1, got2, got3, rows, correlator):
    own = ints[11]
    mine = pl.ds(pl.multiple_of(own * 32, 32), 32)
    for part in range(2):
        rows[own, part] = phi[part, mine, :]
    sums = [jnp.sum(pair[...], axis=1, keepdims=True)]
    for d, got in enumerate((got1, got2, got3), 1):
        rows[(own + 4 - d) & 3] = got[8:72].astype(BF).reshape(2, 32, 128)
        sums.append(jnp.sum(got[0:8], axis=1, keepdims=True))
    sub = lax.broadcasted_iota(jnp.int32, (2, NSRC), 0)
    lane = lax.broadcasted_iota(jnp.int32, (2, NSRC), 1)
    for m in range(2):
        for k in range(2):
            total = jnp.zeros((8, 1), F32)
            for d, value in enumerate(sums):
                total = jnp.where(((own + 4 - d) & 3) == 2 * m + k, value, total)
            block = jnp.zeros((2, NSRC), F32)
            for s in range(NSRC):
                for part in range(2):
                    value = jnp.broadcast_to(total[2 * s + part : 2 * s + part + 1], (2, NSRC))
                    block = jnp.where((sub == part) & (lane == s), value, block)
            correlator[m, k] = block


def half_kernel(ints, keep, got, mine, other):
    chip = ints[11] >> 1
    mine[...] = keep[chip] + got[chip]
    other[...] = (keep[1 - chip] + got[1 - chip]).astype(BF)


def phi_kernel(mine, got, phi):
    total = mine[...] + got[...].astype(F32)
    phi[...] = (total * (1.0 / math.sqrt(12.0 * LX * LY * 16))).astype(BF)


def pick_kernel(sources, chunks, out):
    for s in range(NSRC):
        out[s] = chunks[sources[s] >> 1]


def spread_kernel(ints, sources, mine, other, out):
    for s in range(NSRC):
        value = jnp.where((sources[s] & 1) == ints[12], mine[s], other[s])
        for place in range(32):
            out[place, s] = value


def loop_kernel(phi, whole, *refs, start):
    first = jnp.concatenate(
        [
            jnp.concatenate([phi[0], phi[1]], axis=1),
            jnp.concatenate([phi[1], -phi[0]], axis=1),
        ],
        axis=0,
    )
    out = refs[-1]
    for s in range(NSRC):
        piece, at = (0, 0) if s == 0 else (1, s - 1)
        taus = [(ref, at) for ref in refs[piece:-1:2]]
        if start:
            total = jnp.zeros((128, 256), F32)
            taus.append((whole, s))
        else:
            total = jnp.concatenate([whole[s, 0], whole[s, 1]], axis=1)
        for tau, at in taus:
            pairs = [(tau[at, beta, 0], tau[at, beta, 1]) for beta in range(4)]
            left = jnp.concatenate([jnp.concatenate(pair, axis=0) for pair in pairs], axis=1)
            mid = lax.dot_general(
                left, first, (((0,), (0,)), ((), ())), preferred_element_type=F32
            ).astype(BF)
            mid = jnp.concatenate([mid[beta * 128 : beta * 128 + 128] for beta in range(4)], axis=1)
            second = jnp.concatenate(
                [
                    jnp.concatenate(row, axis=1)
                    for tr, ti in pairs
                    for row in ((tr, ti), (-ti, tr))
                ],
                axis=0,
            )
            total = total + dot_nn(mid, second)
        out[s, 0] = total[:, :128]
        out[s, 1] = total[:, 128:]


def close_kernel(ints, looped, spread, phi, pair, send1, send2, send3):
    for s in range(NSRC):
        src_re = spread[0:16, s].astype(F32).reshape(128, 128)
        src_im = spread[16:32, s].astype(F32).reshape(128, 128)
        yr, yi = looped[s, 0], looped[s, 1]
        re = jnp.sum(yr * src_re + yi * src_im, axis=0, keepdims=True)
        im = jnp.sum(yi * src_re - yr * src_im, axis=0, keepdims=True)
        pair[2 * s : 2 * s + 1, :] = re * (1.0 / (8.0 * 128))
        pair[2 * s + 1 : 2 * s + 2, :] = im * (1.0 / (8.0 * 128))
    for d, send in enumerate((send1, send2, send3), 1):
        send[0:8] = pair[...]
        rows = pl.ds(pl.multiple_of(((ints[11] + d) & 3) * 32, 32), 32)
        for part in range(2):
            send[8 + 32 * part : 40 + 32 * part] = phi[part, rows, :].astype(F32)


VMEM = pl.BlockSpec(memory_space=pltpu.VMEM)
SMEM = pl.BlockSpec(memory_space=pltpu.SMEM)


def call(kernel, outs, inputs, scratch, flops, moved):
    return pl.pallas_call(
        kernel,
        out_shape=outs,
        in_specs=[SMEM if x.ndim == 1 else VMEM for x in inputs],
        out_specs=jax.tree.map(lambda _: VMEM, outs),
        scratch_shapes=scratch,
        compiler_params=pltpu.CompilerParams(vmem_limit_bytes=40 * 2**20),
        cost_estimate=pl.CostEstimate(flops=flops, bytes_accessed=moved, transcendentals=0),
    )(*inputs)


def partner(value, axis, distance=1):
    n = math.prod(lax.axis_size(name) for name in ([axis] if isinstance(axis, str) else axis))
    return lax.ppermute(value, axis, [((i + distance) % n, i) for i in range(n)])


def shaped(*shape, dtype=F32):
    return jax.ShapeDtypeStruct(shape, dtype)


def on_device(eigvecs, gauge_links, peramb, momenta, disp_paths, sources):
    eig = eigvecs[0]
    depth = eig.shape[2]
    own = lax.axis_index("xl") * 2 + lax.axis_index("c")
    tau = peramb[0, :, 0]
    piece = [shaped(n, *tau.shape[1:], dtype=BF) for n in (1, 3)]
    links = gauge_links[0].reshape(54, depth, LX * LY)
    lowest, head = pl.pallas_call(
        pieces_kernel,
        out_shape=(shaped(2, 3, 256, 128, dtype=BF), piece[0]),
        in_specs=[pl.BlockSpec(memory_space=pl.ANY)] * 2,
        out_specs=(VMEM,) * 2,
        scratch_shapes=[pltpu.SemaphoreType.DMA((7,))],
    )(eig, tau)
    halo = partner(lowest, GZ)
    near = partner(tau, "c")
    far = [partner(head, "xl")]
    ints = jnp.concatenate(
        [
            momenta.reshape(6),
            disp_paths.reshape(4),
            jnp.stack([own * depth, own, lax.axis_index("xh")]).astype(jnp.int32),
        ]
    )
    acc, phased, edge_links = call(
        local_kernel,
        (shaped(4, 512, 256), shaped(2, 512, 768, dtype=BF), shaped(1, 54, 256)),
        (ints, eig, links),
        [
            pltpu.VMEM((4, 6, 128, 256), F32),
            pltpu.VMEM((2, 6, 128, 256), F32),
            pltpu.VMEM((3, 256, 768), BF),
            pltpu.VMEM((2, 256, 256), BF),
            pltpu.VMEM((depth, 54, 256), F32),
        ],
        4 * 10**9,
        5 * 10**6,
    )
    far[0], acc = lax.optimization_barrier((far[0], acc))
    keep, send, rest = call(
        edge_kernel,
        (shaped(2, 2, 128, 128), shaped(2, 2, 128, 128), piece[1]),
        (ints, halo, edge_links, acc, phased, tau),
        [pltpu.VMEM((6, 128, 256), F32), pltpu.VMEM((256, 768), BF)],
        5 * 10**8,
        5 * 10**6,
    )
    whole = shaped(2, 128, 128)
    mine, other = call(half_kernel, (whole, shaped(2, 128, 128, dtype=BF)), (ints, keep, partner(send, "c")), [], 10**5, 10**6)
    arrived = partner(other, "xl")
    last, arrived = lax.optimization_barrier((rest, arrived))
    far.append(partner(last, "xl"))
    phi = call(phi_kernel, shaped(2, 128, 128, dtype=BF), (mine, arrived), [], 10**5, 10**6)

    chunks = lax.all_to_all(phi.reshape(32, 8, 128), YZ, 0, 0, tiled=True)
    four = shaped(NSRC, 8, 128, dtype=BF)
    picked = call(pick_kernel, four, (sources, chunks), [], 10**4, 10**5)
    crossed = partner(picked, "xh")
    phi, _ = lax.optimization_barrier((phi, picked))

    def loop(start, total, *taus):
        return call(
            functools.partial(loop_kernel, start=start),
            shaped(NSRC, 2, 128, 128),
            (phi, total, *taus),
            [],
            5 * 10**8 * (1 + start),
            2 * 10**6 * (1 + start),
        )

    looped = loop(True, near, head, rest)
    looped, far = lax.optimization_barrier((looped, far))
    diagonal = [partner(one, "c") for one in far]
    looped = loop(False, looped, *far)
    looped = loop(False, looped, *diagonal)
    looped, crossed = lax.optimization_barrier((looped, crossed))
    spread = call(
        spread_kernel,
        shaped(32, NSRC, 8, 128, dtype=BF),
        (ints, sources, picked, crossed),
        [],
        10**4,
        10**5,
    )
    spread = lax.all_to_all(spread, YZ, 0, 0, tiled=True)
    pair, *sends = call(
        close_kernel,
        (shaped(8, 128), *[shaped(72, 128)] * 3),
        (ints, looped, spread, phi),
        [],
        10**5,
        10**6,
    )
    rows, correlator = call(
        final_kernel,
        (shaped(4, 2, 32, 128, dtype=BF), shaped(2, 2, 2, NSRC)),
        (ints, pair, phi, *[partner(send, GZ, -d) for d, send in enumerate(sends, 1)]),
        [],
        10**5,
        10**6,
    )
    correlator = jnp.transpose(correlator, (3, 0, 1, 2))[:, None]
    return rows.reshape(1, 2, 2, 2, 32, 128), correlator


def solution(mesh):
    fine = Mesh(np.asarray(mesh.devices).reshape(4, 8, 2, 2, 2), (*TA, *GZ))
    placed = (
        P(TA, None, None, GZ, None, None),
        P(TA, None, None, None, None, GZ, None),
        P(TA, None, GZ, None, None, None, None),
        P(),
        P(),
        P(),
    )
    return jax.shard_map(
        on_device,
        mesh=fine,
        in_specs=placed,
        out_specs=(P(TA, None, None, None, GZ, None), P(None, TA, None, None, None)),
        check_vma=False,
    )
```

```python
import functools
import math

import jax
import jax.numpy as jnp
import numpy as np
from jax import lax
from jax.experimental import pallas as pl
from jax.experimental.pallas import tpu as pltpu
from jax.sharding import Mesh
from jax.sharding import PartitionSpec as P

LX = 16
LY = 16
NSRC = 4
BF = jnp.bfloat16
F32 = jnp.float32
NT_DIMS = (((1,), (1,)), ((), ()))
TA = ("y", "z", "xh")
YZ = ("y", "z")
GZ = ("xl", "c")


def dot_nt(a, b):
    return lax.dot_general(a, b, NT_DIMS, preferred_element_type=F32)


def dot_nn(a, b):
    return jnp.dot(a, b, preferred_element_type=F32)


def shift_matrix(direction):
    row = lax.broadcasted_iota(jnp.int32, (256, 256), 0)
    col = lax.broadcasted_iota(jnp.int32, (256, 256), 1)
    if direction == 0:
        target = (col + LY) & 255
    else:
        target = (col & ~(LY - 1)) | ((col + 1) & (LY - 1))
    return jnp.where(row == target, 1.0, 0.0).astype(F32).astype(BF)


def unit_matrix(n):
    row = lax.broadcasted_iota(jnp.int32, (n, n), 0)
    col = lax.broadcasted_iota(jnp.int32, (n, n), 1)
    return jnp.where(row == col, 1.0, 0.0).astype(F32).astype(BF)


def transport(links, z, direction, source, target):
    for half in range(2):
        lanes = pl.ds(half * 128, 128)
        coef = [
            [
                [
                    jnp.broadcast_to(
                        links[z, pl.ds(direction * 18 + a * 6 + b * 2 + part, 1), lanes], (8, 128)
                    )
                    for part in range(2)
                ]
                for b in range(3)
            ]
            for a in range(3)
        ]

        for step in range(8):
            parts = []
            for sub in range(2):
                at = pl.ds(step * 16 + sub * 8, 8)
                vec = [[source(part * 3 + b, at, lanes) for b in range(3)] for part in range(2)]
                out = []
                for a in range(3):
                    re = im = None
                    for b in range(3):
                        ur, ui = coef[a][b]
                        tr = ur * vec[0][b] - ui * vec[1][b]
                        ti = ur * vec[1][b] + ui * vec[0][b]
                        re = tr if re is None else re + tr
                        im = ti if im is None else im + ti
                    out.append((re, im))
                parts.append(out)
            for a in range(3):
                for part in range(2):
                    block = jnp.concatenate([parts[0][a][part], parts[1][a][part]], axis=0)
                    start = part * 128 + step * 16
                    target[pl.ds(start, 16), pl.ds(a * 256 + half * 128, 128)] = block.astype(BF)


def phase_rows(ints, row, plane):
    site = lax.broadcasted_iota(jnp.int32, (8, 256), 1)
    x1 = site >> 4
    x2 = site & (LY - 1)
    steps = ints[row * 3] * x1 + ints[row * 3 + 1] * x2 + ints[row * 3 + 2] * plane
    angle = (steps & 15).astype(F32) * (2.0 * math.pi / 16.0)
    return jnp.cos(angle), jnp.sin(angle)


def phase_plane(ints, z, vt, phased):
    for m in range(2):
        cosine, sine = phase_rows(ints, m, ints[10] + z)
        for half in range(2):
            lanes = pl.ds(half * 128, 128)
            cs = cosine[:, half * 128 : half * 128 + 128]
            sn = sine[:, half * 128 : half * 128 + 128]
            cs = jnp.concatenate([cs] * 2, axis=0)
            sn = jnp.concatenate([sn] * 2, axis=0)
            for step in range(8):
                at = pl.ds(step * 16, 16)
                for a in range(3):
                    re = vt[z, a, at, lanes]
                    im = vt[z, 3 + a, at, lanes]
                    rc, rs, ic, js = re * cs, re * sn, im * cs, im * sn
                    to = pl.ds(a * 256 + half * 128, 128)
                    for block, value in enumerate((rc - js, -(rs + ic), rc + js, rs - ic)):
                        phased[m, pl.ds(block * 128 + step * 16, 16), to] = value.astype(BF)


def local_kernel(ints, eig, narrow, acc, phased, edge_links, vt, vs, field, perm, links):
    unit = unit_matrix(128)
    perm[0] = shift_matrix(0)
    perm[1] = shift_matrix(1)
    wide = narrow[...].astype(F32)
    for z in range(4):
        links[z] = wide[:, z, :]
    edge_links[0] = links[3]

    def load(z, _):
        for comp in range(6):
            vt[z, comp] = dot_nt(unit, eig[comp // 3, comp % 3, z])
        return 0
    lax.fori_loop(0, 4, load, 0)
    acc[...] = jnp.zeros_like(acc)
    which = [jnp.where(ints[6 + 2 * m] == 3, ints[7 + 2 * m], ints[6 + 2 * m]) - 1 for m in range(2)]
    def plane(z, last):
        phase_plane(ints, z, vt, phased)
        for direction in range(2):
            vs[direction] = dot_nn(vt[z].reshape(768, 256).astype(BF), perm[direction]).reshape(6, 128, 256)
        for direction in range(2):
            transport(links, z, direction, lambda comp, at, lanes: vs[direction, comp, at, lanes], field.at[direction])
        if not last:
            transport(links, z, 2, lambda comp, at, lanes: vt[z + 1, comp, at, lanes], field.at[2])
            t = dot_nt(phased[...].reshape(1024, 768), field[2])
            acc[0] += t[:512]
            acc[2] += t[512:]
        for m in range(2):
            acc[2 * m + 1] += dot_nt(phased[m], field[which[m]])
        return 0
    lax.fori_loop(0, 3, lambda z, _: plane(z, False), 0)
    plane(3, True)


def edge_kernel(ints, halo, links, acc, phased, tau, keep, send, rest, vt, field):
    unit = unit_matrix(128)
    for comp in range(6):
        vt[comp] = dot_nt(unit, halo[comp // 3, comp % 3])
    transport(links, links.shape[0] - 1, 2, lambda comp, at, lanes: vt[comp, at, lanes], field)
    rest[...] = tau[1:4]
    core = ints[11] & 1
    edge = dot_nt(phased[...].reshape(1024, 768), field[...])
    for m in range(2):
        along = jnp.where(ints[6 + 2 * m] == 3, 0, 1)
        for o in range(2):
            t = acc[2 * m + o]
            if o == 0:
                t = t + edge[512 * m : 512 * m + 512]
                slot = along
            else:
                slot = 1 - along
            direction = ints[6 + 2 * m + slot] - 1
            turn = jnp.full((8, 128), ints[3 * m + direction] & 15, jnp.int32).astype(F32)
            turn = turn * (2.0 * math.pi / 16.0)
            cd = jnp.cos(turn)[:1]
            sd = jnp.sin(turn)[:1]
            ar = t[0:128, 0:128] - t[128:256, 128:256]
            ai = t[0:128, 128:256] + t[128:256, 0:128]
            br = (t[256:384, 0:128] - t[384:512, 128:256]).T
            bi = (t[256:384, 128:256] + t[384:512, 0:128]).T
            re = ar - cd * br + sd * bi
            im = ai + sd * br + cd * bi

            def store(ref, m=m, re=re, im=im):
                ref[m, 0] = re
                ref[m, 1] = im

            pl.when(slot == core)(functools.partial(store, keep))
            pl.when(slot != core)(functools.partial(store, send))


def pieces_kernel(eig, tau, lowest, head, sems):
    moves = [(eig.at[part, a, 0], lowest.at[part, a]) for part in range(2) for a in range(3)]
    moves.append((tau.at[pl.ds(0, 1)], head))
    copies = [pltpu.make_async_copy(*move, sems.at[n]) for n, move in enumerate(moves)]
    for copy in copies:
        copy.start()
    for copy in copies:
        copy.wait()


def final_kernel(ints, pair, phi, got1, got2, got3, rows, correlator):
    own = ints[11]
    mine = pl.ds(pl.multiple_of(own * 32, 32), 32)
    for part in range(2):
        rows[own, part] = phi[part, mine, :]
    sums = [jnp.sum(pair[...], axis=1, keepdims=True)]
    for d, got in enumerate((got1, got2, got3), 1):
        rows[(own + 4 - d) & 3] = got[8:72].astype(BF).reshape(2, 32, 128)
        sums.append(jnp.sum(got[0:8], axis=1, keepdims=True))
    sub = lax.broadcasted_iota(jnp.int32, (2, NSRC), 0)
    lane = lax.broadcasted_iota(jnp.int32, (2, NSRC), 1)
    for m in range(2):
        for k in range(2):
            total = jnp.zeros((8, 1), F32)
            for d, value in enumerate(sums):
                total = jnp.where(((own + 4 - d) & 3) == 2 * m + k, value, total)
            block = jnp.zeros((2, NSRC), F32)
            for s in range(NSRC):
                for part in range(2):
                    value = jnp.broadcast_to(total[2 * s + part : 2 * s + part + 1], (2, NSRC))
                    block = jnp.where((sub == part) & (lane == s), value, block)
            correlator[m, k] = block


def half_kernel(ints, keep, got, mine, other):
    chip = ints[11] >> 1
    mine[...] = keep[chip] + got[chip]
    other[...] = (keep[1 - chip] + got[1 - chip]).astype(BF)


def phi_kernel(mine, got, phi):
    total = mine[...] + got[...].astype(F32)
    phi[...] = (total * (1.0 / math.sqrt(12.0 * LX * LY * 16))).astype(BF)


def pick_kernel(sources, chunks, out):
    for s in range(NSRC):
        out[s] = chunks[sources[s] >> 1]


def spread_kernel(ints, sources, mine, other, out):
    for s in range(NSRC):
        value = jnp.where((sources[s] & 1) == ints[12], mine[s], other[s])
        for place in range(32):
            out[place, s] = value


def loop_kernel(phi, whole, *refs, start):
    first = jnp.concatenate(
        [
            jnp.concatenate([phi[0], phi[1]], axis=1),
            jnp.concatenate([phi[1], -phi[0]], axis=1),
        ],
        axis=0,
    )
    out = refs[-1]
    for s in range(NSRC):
        piece, at = (0, 0) if s == 0 else (1, s - 1)
        taus = [(ref, at) for ref in refs[piece:-1:2]]
        if start:
            total = jnp.zeros((128, 256), F32)
            taus.append((whole, s))
        else:
            total = jnp.concatenate([whole[s, 0], whole[s, 1]], axis=1)
        for tau, at in taus:
            pairs = [(tau[at, beta, 0], tau[at, beta, 1]) for beta in range(4)]
            left = jnp.concatenate([jnp.concatenate(pair, axis=0) for pair in pairs], axis=1)
            mid = lax.dot_general(
                left, first, (((0,), (0,)), ((), ())), preferred_element_type=F32
            ).astype(BF)
            mid = jnp.concatenate([mid[beta * 128 : beta * 128 + 128] for beta in range(4)], axis=1)
            second = jnp.concatenate(
                [
                    jnp.concatenate(row, axis=1)
                    for tr, ti in pairs
                    for row in ((tr, ti), (-ti, tr))
                ],
                axis=0,
            )
            total = total + dot_nn(mid, second)
        out[s, 0] = total[:, :128]
        out[s, 1] = total[:, 128:]


def close_kernel(ints, looped, spread, phi, pair, send1, send2, send3):
    for s in range(NSRC):
        src_re = spread[0:16, s].astype(F32).reshape(128, 128)
        src_im = spread[16:32, s].astype(F32).reshape(128, 128)
        yr, yi = looped[s, 0], looped[s, 1]
        re = jnp.sum(yr * src_re + yi * src_im, axis=0, keepdims=True)
        im = jnp.sum(yi * src_re - yr * src_im, axis=0, keepdims=True)
        pair[2 * s : 2 * s + 1, :] = re * (1.0 / (8.0 * 128))
        pair[2 * s + 1 : 2 * s + 2, :] = im * (1.0 / (8.0 * 128))
    for d, send in enumerate((send1, send2, send3), 1):
        send[0:8] = pair[...]
        rows = pl.ds(pl.multiple_of(((ints[11] + d) & 3) * 32, 32), 32)
        for part in range(2):
            send[8 + 32 * part : 40 + 32 * part] = phi[part, rows, :].astype(F32)


VMEM = pl.BlockSpec(memory_space=pltpu.VMEM)
SMEM = pl.BlockSpec(memory_space=pltpu.SMEM)


def call(kernel, outs, inputs, scratch, flops, moved):
    return pl.pallas_call(
        kernel,
        out_shape=outs,
        in_specs=[SMEM if x.ndim == 1 else VMEM for x in inputs],
        out_specs=jax.tree.map(lambda _: VMEM, outs),
        scratch_shapes=scratch,
        compiler_params=pltpu.CompilerParams(vmem_limit_bytes=(40 if kernel is local_kernel else 20) * 2**20),
        cost_estimate=pl.CostEstimate(flops=flops, bytes_accessed=moved, transcendentals=0),
    )(*inputs)


def partner(value, axis, distance=1):
    n = math.prod(lax.axis_size(name) for name in ([axis] if isinstance(axis, str) else axis))
    return lax.ppermute(value, axis, [((i + distance) % n, i) for i in range(n)])


def shaped(*shape, dtype=F32):
    return jax.ShapeDtypeStruct(shape, dtype)


def on_device(eigvecs, gauge_links, peramb, momenta, disp_paths, sources):
    eig = eigvecs[0]
    depth = eig.shape[2]
    own = lax.axis_index("xl") * 2 + lax.axis_index("c")
    tau = peramb[0, :, 0]
    piece = [shaped(n, *tau.shape[1:], dtype=BF) for n in (1, 3)]
    links = gauge_links[0].reshape(54, depth, LX * LY)
    lowest, head = pl.pallas_call(
        pieces_kernel,
        out_shape=(shaped(2, 3, 256, 128, dtype=BF), piece[0]),
        in_specs=[pl.BlockSpec(memory_space=pl.ANY)] * 2,
        out_specs=(VMEM,) * 2,
        scratch_shapes=[pltpu.SemaphoreType.DMA((7,))],
    )(eig, tau)
    halo = partner(lowest, GZ)
    near = partner(tau, "c")
    far = [partner(head, "xl")]
    ints = jnp.concatenate(
        [
            momenta.reshape(6),
            disp_paths.reshape(4),
            jnp.stack([own * depth, own, lax.axis_index("xh")]).astype(jnp.int32),
        ]
    )
    acc, phased, edge_links = call(
        local_kernel,
        (shaped(4, 512, 256), shaped(2, 512, 768, dtype=BF), shaped(1, 54, 256)),
        (ints, eig, links),
        [
            pltpu.VMEM((4, 6, 128, 256), F32),
            pltpu.VMEM((2, 6, 128, 256), F32),
            pltpu.VMEM((3, 256, 768), BF),
            pltpu.VMEM((2, 256, 256), BF),
            pltpu.VMEM((depth, 54, 256), F32),
        ],
        4 * 10**9,
        5 * 10**6,
    )
    far[0], acc = lax.optimization_barrier((far[0], acc))
    keep, send, rest = call(
        edge_kernel,
        (shaped(2, 2, 128, 128), shaped(2, 2, 128, 128), piece[1]),
        (ints, halo, edge_links, acc, phased, tau),
        [pltpu.VMEM((6, 128, 256), F32), pltpu.VMEM((256, 768), BF)],
        5 * 10**8,
        5 * 10**6,
    )
    whole = shaped(2, 128, 128)
    mine, other = call(half_kernel, (whole, shaped(2, 128, 128, dtype=BF)), (ints, keep, partner(send, "c")), [], 10**5, 10**6)
    arrived = partner(other, "xl")
    last, arrived = lax.optimization_barrier((rest, arrived))
    far.append(partner(last, "xl"))
    phi = call(phi_kernel, shaped(2, 128, 128, dtype=BF), (mine, arrived), [], 10**5, 10**6)

    chunks = lax.all_to_all(phi.reshape(32, 8, 128), YZ, 0, 0, tiled=True)
    four = shaped(NSRC, 8, 128, dtype=BF)
    picked = call(pick_kernel, four, (sources, chunks), [], 10**4, 10**5)
    crossed = partner(picked, "xh")
    phi, _ = lax.optimization_barrier((phi, picked))

    def loop(start, total, *taus):
        return call(
            functools.partial(loop_kernel, start=start),
            shaped(NSRC, 2, 128, 128),
            (phi, total, *taus),
            [],
            5 * 10**8 * (1 + start),
            2 * 10**6 * (1 + start),
        )

    looped = loop(True, near, head, rest)
    looped, far = lax.optimization_barrier((looped, far))
    diagonal = [partner(one, "c") for one in far]
    looped = loop(False, looped, *far)
    looped = loop(False, looped, *diagonal)
    looped, crossed = lax.optimization_barrier((looped, crossed))
    spread = call(
        spread_kernel,
        shaped(32, NSRC, 8, 128, dtype=BF),
        (ints, sources, picked, crossed),
        [],
        10**4,
        10**5,
    )
    spread = lax.all_to_all(spread, YZ, 0, 0, tiled=True)
    pair, *sends = call(
        close_kernel,
        (shaped(8, 128), *[shaped(72, 128)] * 3),
        (ints, looped, spread, phi),
        [],
        10**5,
        10**6,
    )
    rows, correlator = call(
        final_kernel,
        (shaped(4, 2, 32, 128, dtype=BF), shaped(2, 2, 2, NSRC)),
        (ints, pair, phi, *[partner(send, GZ, -d) for d, send in enumerate(sends, 1)]),
        [],
        10**5,
        10**6,
    )
    correlator = jnp.transpose(correlator, (3, 0, 1, 2))[:, None]
    return rows.reshape(1, 2, 2, 2, 32, 128), correlator


def solution(mesh):
    fine = Mesh(np.asarray(mesh.devices).reshape(4, 8, 2, 2, 2), (*TA, *GZ))
    placed = (
        P(TA, None, None, GZ, None, None),
        P(TA, None, None, None, None, GZ, None),
        P(TA, None, GZ, None, None, None, None),
        P(),
        P(),
        P(),
    )
    return jax.shard_map(
        on_device,
        mesh=fine,
        in_specs=placed,
        out_specs=(P(TA, None, None, None, GZ, None), P(None, TA, None, None, None)),
        check_vma=False,
    )
```
